512 devices in a mesh: dp: 64 (over z, y), owner: 8 (over x, core).
Axes of the slice: x: 4, y: 4, z: 16, core: 2. Of those that a mesh axis runs over, the one named last changes fastest.
Arguments:
- query_out: bfloat16 [512, 16384], P('dp', 'owner'), may hold values from -6 to 6
- query_in: bfloat16 [512, 8192], P('dp'), may hold values from -6 to 6
- train_out: bfloat16 [512, 16384], P('dp', 'owner'), may hold values from -6 to 6
- train_in: bfloat16 [512, 8192], P('dp'), may hold values from -6 to 6
- basis_out: bfloat16 [96, 256, 256], P('owner'), may hold values from -1 to 1, as said below
- basis_in: bfloat16 [64, 128, 128], P('dp'), may hold values from -1 to 1, as said below
- eigvals: float32 [24576, 8192], P('owner', 'dp'), may hold values from 0.1 to 10
- owner_map: int32 [64], replicated, may hold values from 0 to 7, as said below
Outputs:
- scores: float32 [8, 32], replicated
The draws below stay inside these ranges and needn't reach their ends.
Inputs may be any that keep to these rules, and one draw needn't show every extreme that they name: owner_map[b] is the owner of hidden block b. Blocks form ranges of 8 in order; a block of range r is owned by r or by r xor 1. Of two such partner owners one holds exactly 12 blocks and keeps 12 // 2 of its own range, the other holds 4 blocks and keeps 8 - 12 // 2 of its own range. `basis_out`: each [256, 256] block is an orthogonal matrix rounded to bfloat16; block o * 12 + s belongs to the s-th block, in block order, that owner o holds; blocks past an owner's count are not read. `basis_in`: each [128, 128] block is an orthogonal matrix rounded to bfloat16.
All inputs are finite; a program needn't handle non-finite values.
Results may differ from the reference program's by a relative error of at most 0.0067.
Values may be sent and summed in bfloat16 or wider, within the bound.
No kernel may reach another device: no remote copies, remote signals or barrier semaphores. Data moves between devices by JAX's collectives and lax.ppermute only.
A program may use at most 64 MiB of HBM per device.

```python
import math
import jax
import jax.numpy as jnp
from jax import lax

D = 8192
BK = 256
BA = 128
BLK_OWN = 8
CAP = 12
NQ = 8
ET = 16
F = 16384
NB = 64
QTOK = 512
QT = 64
TT = 512
NE = 32
N_OWNER = 8


def orthogonal_blocks(key, block_count, block_size):
    normal = jax.random.normal(key, (block_count, block_size, block_size), jnp.float32)
    basis_q, upper_part = jnp.linalg.qr(normal)
    sign_fix = jnp.sign(jnp.diagonal(upper_part, axis1=1, axis2=2))
    sign_fix = jnp.where(sign_fix == 0, 1.0, sign_fix)
    return basis_q * sign_fix[:, None, :]


def draw_basis_out(key, part):
    return orthogonal_blocks(jax.random.fold_in(key, 11), N_OWNER * CAP, BK).astype(jnp.bfloat16)


def draw_basis_in(key, part):
    return orthogonal_blocks(jax.random.fold_in(key, 13), D // BA, BA).astype(jnp.bfloat16)


def draw_owner_map(key, part):
    pair_total = N_OWNER // 2
    heavy_bits = jax.random.randint(jax.random.fold_in(key, 21), (pair_total,), 0, 2).astype(jnp.int32)
    range_ids = jnp.arange(N_OWNER, dtype=jnp.int32)
    shuffled = jax.vmap(lambda range_index: jax.random.permutation(jax.random.fold_in(key, 1000 + range_index), BLK_OWN))(range_ids)
    position = jnp.argsort(shuffled, axis=1).astype(jnp.int32)
    heavy = range_ids // 2 * 2 + heavy_bits[range_ids // 2]
    keep_count = jnp.where(range_ids == heavy, CAP // 2, BLK_OWN - CAP // 2)
    partner = jnp.bitwise_xor(range_ids, 1)
    owners = jnp.where(position < keep_count[:, None], range_ids[:, None], partner[:, None])
    return owners.reshape(N_OWNER * BLK_OWN).astype(jnp.int32)


def block_levels(stream_key, shape, cuts, low, high):
    loudness, own = 1.0, jax.random.fold_in(stream_key, 6)
    for dim, shards_of in cuts:
        draws = jnp.exp(jax.random.uniform(jax.random.fold_in(own, dim), (shards_of,), jnp.float32, low / len(cuts), high / len(cuts)))
        loudness = loudness * jnp.repeat(draws, shape[dim] // shards_of).reshape([-1 if axis == dim else 1 for axis in range(len(shape))])
    return loudness


def normal_values(stream_key, extent, spread, bound, shards=(), held_as=jnp.bfloat16):
    loudness = block_levels(stream_key, extent, shards, -0.22, 0.18) if shards else 1.0
    array = jax.random.normal(stream_key, extent, jnp.float32) * spread * loudness
    return jnp.minimum(jnp.maximum(array, -bound), bound).astype(held_as)


def setup_inputs(seed: int = 0) -> dict:
    keys = jax.random.split(jax.random.key(seed), 9)
    query_out = normal_values(keys[0], (QTOK, F), 1.0, 6.0, ((0, 64), (1, 8)))
    query_in = normal_values(keys[1], (QTOK, D), 1.0, 6.0, ((0, 64),))
    train_out = normal_values(keys[2], (TT, F), 1.0, 6.0, ((0, 64), (1, 8)))
    train_in = normal_values(keys[3], (TT, D), 1.0, 6.0, ((0, 64),))
    basis_out = draw_basis_out(jax.random.fold_in(keys[8], 71), 0)
    basis_in = draw_basis_in(jax.random.fold_in(keys[8], 71), 0)
    eigvals = jnp.clip(jnp.exp(math.log(10.0) - 4.6051702 * jax.random.uniform(keys[6], (N_OWNER * CAP * BK, D), jnp.float32) ** block_levels(keys[6], (N_OWNER * CAP * BK, D), ((0, 8), (1, 64)), -0.2, 0.2)), 0.1, 10.0)
    owner_map = draw_owner_map(jax.random.fold_in(keys[8], 71), 0)
    return {"query_out": query_out, "query_in": query_in, "train_out": train_out, "train_in": train_in, "basis_out": basis_out, "basis_in": basis_in, "eigvals": eigvals, "owner_map": owner_map}


DAMPING = 0.1

def rotate_columns(values, basis_in):
    token_count = values.shape[0]
    blocks = values.reshape(token_count, D // BA, BA).astype(jnp.float32)
    turned = jnp.einsum('tnb,nbc->tnc', blocks, basis_in.astype(jnp.float32))
    return turned.astype(jnp.bfloat16).reshape(token_count, D)

def reference(query_out, query_in, train_out, train_in, basis_out, basis_in, eigvals, owner_map):
    block_ids = jnp.arange(NB, dtype=jnp.int32)
    same_owner = owner_map[None, :] == owner_map[:, None]
    earlier = block_ids[None, :] < block_ids[:, None]
    slot_rank = lax.optimization_barrier(jnp.sum((same_owner & earlier).astype(jnp.int32), axis=1)).astype(jnp.int32)
    slot_index = (owner_map * CAP + slot_rank).astype(jnp.int32)
    query_act = rotate_columns(query_in, basis_in)
    train_inputs = train_in.reshape(NE, ET, D).astype(jnp.float32)
    basis_in_wide = basis_in.astype(jnp.float32)

    def one_block(block_index):
        slot_now = slot_index[block_index]
        eig_basis = lax.dynamic_index_in_dim(basis_out, slot_now, 0, keepdims=False)
        first_unit = (block_index * BK).astype(jnp.int32)
        query_block = lax.dynamic_slice_in_dim(query_out, first_unit, BK, 1)
        query_rot = jnp.dot(query_block.astype(jnp.float32), eig_basis.astype(jnp.float32), preferred_element_type=jnp.float32).astype(jnp.bfloat16)
        shifted = lax.dynamic_slice_in_dim(eigvals, (slot_now * BK).astype(jnp.int32), BK, 0) + DAMPING
        train_block = lax.dynamic_slice_in_dim(train_out, first_unit, BK, 1).reshape(NE, ET, BK).astype(jnp.float32)
        example_grad = jnp.einsum('etk,etd->ekd', train_block, train_inputs)

        def one_query(query_index):
            first_row = (query_index * QT).astype(jnp.int32)
            left_side = lax.dynamic_slice_in_dim(query_rot, first_row, QT, 0)
            right_side = lax.dynamic_slice_in_dim(query_act, first_row, QT, 0)
            moment = jnp.dot(left_side.T.astype(jnp.float32), right_side.astype(jnp.float32), preferred_element_type=jnp.float32)
            damped = (moment / shifted).astype(jnp.bfloat16)
            half_back = jnp.einsum('knb,ncb->knc', damped.reshape(BK, D // BA, BA).astype(jnp.float32), basis_in_wide)
            half_back = half_back.astype(jnp.bfloat16).reshape(BK, D)
            precond = jnp.dot(eig_basis.astype(jnp.float32), half_back.astype(jnp.float32), preferred_element_type=jnp.float32).astype(jnp.bfloat16)
            return jnp.einsum('kd,ekd->e', precond.astype(jnp.float32), example_grad)
        return lax.map(one_query, jnp.arange(NQ, dtype=jnp.int32))
    totals = lax.map(one_block, block_ids)
    score_scale = 1.0 / math.sqrt(QT * ET * F * D)
    return lax.optimization_barrier(jnp.sum(totals, axis=0)) * score_scale
```

```python
import math

import jax
import jax.numpy as jnp
from jax import lax
from jax.experimental import pallas as pl
from jax.experimental.pallas import tpu as pltpu
from jax.sharding import Mesh, PartitionSpec as P


NQ = 8
ET = 16
DAMPING = 0.1
NZ, NY, NX, NC = 16, 4, 4, 2
BF = jnp.bfloat16
F32 = jnp.float32
INTERPRET = False


def swap_core(array):
    return lax.ppermute(array, "c", [(0, 1), (1, 0)])


def exchange(array, axis):
    return lax.all_to_all(array, axis, split_axis=0, concat_axis=0, tiled=True)


def prepare(owner_map, place, eigvals, basis_out):
    capacity, bk = basis_out.shape[0], basis_out.shape[1]
    ba = eigvals.shape[1]
    own_blocks = owner_map.shape[0] // (NX * NC)
    mine = own_blocks // NY

    def body(map_ref, place_ref, eig_ref, basis_ref, wk_ref, ws_ref, bk_ref, bs_ref, slot_ref, own_ref):
        x, y, c = place_ref[0], place_ref[1], place_ref[2]
        owner = NC * x + c
        count = jnp.int32(0)
        for p in range(NC * own_blocks):
            is_own = (map_ref[x * (NC * own_blocks) + p] == owner).astype(jnp.int32)
            slot_ref[p] = jnp.minimum(count, capacity - 1)
            own_ref[p] = is_own
            count = count + is_own
        for side, w_out, b_out in ((c, wk_ref, bk_ref), (1 - c, ws_ref, bs_ref)):
            for i in range(own_blocks):
                p = side * own_blocks + i
                start = pl.multiple_of(slot_ref[p] * bk, bk)
                values = 1.0 / (eig_ref[pl.ds(start, bk), :] + DAMPING)
                w_out[i] = jnp.where(own_ref[p] > 0, values, 0.0).astype(BF)
            for k in range(mine):
                p = side * own_blocks + mine * y + k
                block = basis_ref[slot_ref[p]].astype(F32)
                b_out[k] = jnp.where(own_ref[p] > 0, block, 0.0).astype(BF)

    w_shape = jax.ShapeDtypeStruct((own_blocks, bk, ba), BF)
    b_shape = jax.ShapeDtypeStruct((mine, bk, bk), BF)
    smem = pl.BlockSpec(memory_space=pltpu.SMEM)
    vmem = pl.BlockSpec(memory_space=pltpu.VMEM)
    return pl.pallas_call(
        body,
        out_shape=(w_shape, w_shape, b_shape, b_shape),
        in_specs=[smem, smem, vmem, vmem],
        out_specs=(vmem,) * 4,
        scratch_shapes=[pltpu.SMEM((NC * own_blocks,), jnp.int32)] * 2,
        name="prepare",
        interpret=INTERPRET,
    )(owner_map, place, eigvals, basis_out)


def score(place, most, rest, b_keep, b_recv, act, other, weights, scale):
    seg, fdim = rest.shape
    n_tok = NY * seg
    groups = most.shape[0] // seg
    mine, bk = b_keep.shape[0], b_keep.shape[1]
    ba = act.shape[-1]
    ddim = NY * ba
    per = seg // NQ
    half = NY // 2
    w_at = weights.shape[1] - fdim

    def body(place_ref, q_ref, t_ref, bk_ref, br_ref, a_ref, o_ref, w_ref, out_ref, qr, tr, qa, ta, dm, ex):
        first = place_ref[2] == 0
        for b in range(mine):
            cut = slice(bk * b, bk * b + bk)
            basis = (bk_ref[b].astype(F32) + br_ref[b].astype(F32)).astype(BF)
            tail = jnp.dot(t_ref[:, cut], basis, preferred_element_type=F32)
            turned = jnp.dot(q_ref[:, cut], basis, preferred_element_type=F32)
            turned = turned.reshape(NZ, groups, seg // NZ, bk)
            for g in range(groups + 1):
                block = (turned[:, g].reshape(seg, bk) if g < groups else tail).astype(BF)
                if g >= NY:
                    tr[seg * (g - NY) : seg * (g - NY + 1), cut] = block
                    continue
                for q in range(NQ):
                    at = NY * per * q + per * g
                    qr[at : at + per, cut] = block[per * q : per * q + per]

        def spread(q_from, t_from):
            for y in range(NY):
                for j in range(NY):
                    lanes = slice(ba * j, ba * j + ba)
                    ta[seg * y : seg * y + seg, lanes] = t_from[y, j]
                    for q in range(NQ):
                        at = NY * per * q + per * y
                        qa[at : at + per, lanes] = q_from[y, j, per * q : per * q + per]

        @pl.when(first)
        def _():
            spread(a_ref, o_ref)

        @pl.when(jnp.logical_not(first))
        def _():
            spread(o_ref, a_ref)

        for q in range(NQ):
            rows = slice(NY * per * q, NY * per * (q + 1))
            moment = lax.dot_general(
                qr[rows, :], qa[rows, :], (((0,), (0,)), ((), ())), preferred_element_type=F32
            )
            for j in range(NY):
                lanes = slice(ba * j, ba * j + ba)
                dm[q % 2, :, lanes] = (moment[:, lanes] * w_ref[j, w_at:, :].astype(F32)).astype(BF)
            proj = jnp.dot(tr[...], dm[q % 2], preferred_element_type=F32)
            total = jnp.zeros((n_tok, ba), F32)
            for j in range(NY):
                lanes = slice(ba * j, ba * j + ba)
                total = total + proj[:, lanes] * ta[:, lanes].astype(F32)
            parts = jnp.sum(total.reshape(half, 2, NZ, seg // NZ, ba), axis=(1, 3))
            for h in range(half):
                ex[q, pl.ds(h, NZ, stride=half), :] = parts[h]
        out_ref[...] = jnp.sum(ex[...], axis=2) * scale

    smem = pl.BlockSpec(memory_space=pltpu.SMEM)
    vmem = pl.BlockSpec(memory_space=pltpu.VMEM)
    return pl.pallas_call(
        body,
        out_shape=jax.ShapeDtypeStruct((NQ, half * NZ), F32),
        in_specs=[smem] + [vmem] * 7,
        out_specs=vmem,
        scratch_shapes=[
            pltpu.VMEM((n_tok, fdim), BF),
            pltpu.VMEM((n_tok, fdim), BF),
            pltpu.VMEM((n_tok, ddim), BF),
            pltpu.VMEM((n_tok, ddim), BF),
            pltpu.VMEM((2, fdim, ddim), BF),
            pltpu.VMEM((NQ, half * NZ, ba), F32),
        ],
        name="score",
        interpret=INTERPRET,
    )(place, most, rest, b_keep, b_recv, act, other, weights)


def local(query_out, query_in, train_out, train_in, basis_out, basis_in, eigvals, owner_map):
    x, y, c = lax.axis_index("x"), lax.axis_index("y"), lax.axis_index("c")
    ba = basis_in.shape[1]
    tok, units = query_out.shape
    width = query_in.shape[1]
    fdim = units // NY
    ddim = NY * ba
    ids = jnp.arange(4, dtype=jnp.int32)
    place = jnp.where(ids == 0, x, jnp.where(ids == 1, y, c)).astype(jnp.int32)

    both_out = jnp.concatenate([query_out, train_out], 0)
    rows = exchange(both_out.reshape(2 * tok, NY, fdim).transpose(1, 0, 2), "y")
    w_keep, w_send, b_keep, b_send = prepare(owner_map, place, eigvals, basis_out)
    q_rows = rows[:, :tok].reshape(NY * tok, fdim)
    t_rows = rows[:, tok:].reshape(NY * tok, fdim)
    n_ag = (NY - 1) * tok

    half_in = jnp.where(c == 0, query_in, train_in)
    cols = half_in.reshape(tok, NZ, ddim).transpose(1, 0, 2)
    last = jnp.broadcast_to(t_rows[None, n_ag:], (NZ, tok, fdim))
    mixed = exchange(jnp.concatenate([cols, last], 1), "z")
    w_own = (w_keep + swap_core(w_send)).reshape(NY, fdim, ba)
    b_recv = swap_core(b_send)
    most = jnp.concatenate([q_rows, t_rows[:n_ag]], 0)
    mixed, most, w_own, b_recv = lax.optimization_barrier((mixed, most, w_own, b_recv))
    rest = mixed[:, tok:].reshape(NZ * tok, fdim)

    in_cols = mixed[:, :tok].reshape(NZ * tok, NY, ba).transpose(1, 0, 2).reshape(NY * NZ * tok, ba)
    shared = jnp.concatenate([in_cols, basis_in[0]], 0)
    shared = jnp.broadcast_to(shared[None], (NY,) + shared.shape)
    packed = exchange(jnp.concatenate([shared, w_own], 1), "y")
    gathered = lax.all_gather(most, "z", axis=0, tiled=True)
    packed, gathered = lax.optimization_barrier((packed, gathered))

    n_in = NY * NZ * tok
    in_all = packed[:, :n_in].reshape(NY, NY, NZ * tok, ba)
    act = jnp.einsum("yjtb,jbc->yjtc", in_all, packed[:, n_in : n_in + ba], preferred_element_type=F32).astype(BF)
    other = swap_core(act)

    per = NZ * NY * tok // NQ
    hidden = units * NX * NC
    scale = 1.0 / math.sqrt(per * ET * hidden * width)
    scores = score(place, gathered, rest, b_keep, b_recv, act, other, packed, scale)

    flat = scores.reshape(1, -1, 128)
    flat = jnp.sum(exchange(jnp.broadcast_to(flat, (NY * NX * NC,) + flat.shape[1:]), ("y", "x", "c")), axis=0)[None]
    flat = jnp.sum(exchange(jnp.broadcast_to(flat, (NZ,) + flat.shape[1:]), "z"), axis=0)
    return flat.reshape(scores.shape)


def solution(mesh):
    fine = Mesh(mesh.devices.reshape(NZ, NY, NX, NC), ("z", "y", "x", "c"))
    dp, owner = ("z", "y"), ("x", "c")
    in_specs = (
        P(dp, owner),
        P(dp, None),
        P(dp, owner),
        P(dp, None),
        P(owner, None, None),
        P(dp, None, None),
        P(owner, dp),
        P(),
    )
    return jax.shard_map(local, mesh=fine, in_specs=in_specs, out_specs=P(), check_vma=False)
```

```python
import math

import jax
import jax.numpy as jnp
from jax import lax
from jax.experimental import pallas as pl
from jax.experimental.pallas import tpu as pltpu
from jax.sharding import Mesh, PartitionSpec as P


NQ = 8
ET = 16
DAMPING = 0.1
NZ, NY, NX, NC = 16, 4, 4, 2
BF = jnp.bfloat16
F32 = jnp.float32
INTERPRET = False


def swap_core(array):
    return lax.ppermute(array, "c", [(0, 1), (1, 0)])


def exchange(array, axis):
    return lax.all_to_all(array, axis, split_axis=0, concat_axis=0, tiled=True)


def prepare(owner_map, place, eigvals, basis_out):
    capacity, bk = basis_out.shape[0], basis_out.shape[1]
    ba = eigvals.shape[1]
    own_blocks = owner_map.shape[0] // (NX * NC)
    mine = own_blocks // NY

    def body(map_ref, place_ref, eig_ref, basis_ref, wk_ref, ws_ref, bk_ref, bs_ref, slot_ref, own_ref):
        x, y, c = place_ref[0], place_ref[1], place_ref[2]
        owner = NC * x + c
        count = jnp.int32(0)
        for p in range(NC * own_blocks):
            is_own = (map_ref[x * (NC * own_blocks) + p] == owner).astype(jnp.int32)
            slot_ref[p] = jnp.minimum(count, capacity - 1)
            own_ref[p] = is_own
            count = count + is_own
        for side, w_out, b_out in ((c, wk_ref, bk_ref), (1 - c, ws_ref, bs_ref)):
            for i in range(own_blocks):
                p = side * own_blocks + i
                start = pl.multiple_of(slot_ref[p] * bk, bk)
                values = 1.0 / (eig_ref[pl.ds(start, bk), :] + DAMPING)
                w_out[i] = jnp.where(own_ref[p] > 0, values, 0.0).astype(BF)
            for k in range(mine):
                p = side * own_blocks + mine * y + k
                block = basis_ref[slot_ref[p]].astype(F32)
                b_out[k] = jnp.where(own_ref[p] > 0, block, 0.0).astype(BF)

    w_shape = jax.ShapeDtypeStruct((own_blocks, bk, ba), BF)
    b_shape = jax.ShapeDtypeStruct((mine, bk, bk), BF)
    smem = pl.BlockSpec(memory_space=pltpu.SMEM)
    vmem = pl.BlockSpec(memory_space=pltpu.VMEM)
    return pl.pallas_call(
        body,
        out_shape=(w_shape, w_shape, b_shape, b_shape),
        in_specs=[smem, smem, vmem, vmem],
        out_specs=(vmem,) * 4,
        scratch_shapes=[pltpu.SMEM((NC * own_blocks,), jnp.int32)] * 2,
        name="prepare",
        compiler_params=pltpu.CompilerParams(vmem_limit_bytes=24 << 20),
        interpret=INTERPRET,
    )(owner_map, place, eigvals, basis_out)


def score(most, rest, b_keep, b_recv, packed, scale):
    seg, fdim = rest.shape
    n_tok = NY * seg
    groups = most.shape[0] // seg
    mine, bk = b_keep.shape[0], b_keep.shape[1]
    ba = packed.shape[-1]
    ddim = NY * ba
    per = seg // NQ
    half = NY // 2
    basis_at = 2 * NY * seg
    w_at = basis_at + ba

    def body(m_ref, t_ref, bk_ref, br_ref, p_ref, out_ref, qr, tr, qa, ta, dm, ex):
        for b in range(mine):
            cut = slice(bk * b, bk * b + bk)
            basis = (bk_ref[b].astype(F32) + br_ref[b].astype(F32)).astype(BF)
            tail = jnp.dot(t_ref[:, cut], basis, preferred_element_type=F32)
            turned = jnp.dot(m_ref[:, cut], basis, preferred_element_type=F32)
            turned = turned.reshape(NZ, groups, seg // NZ, bk)
            for g in range(groups + 1):
                block = (turned[:, g].reshape(seg, bk) if g < groups else tail).astype(BF)
                if g >= NY:
                    tr[seg * (g - NY) : seg * (g - NY + 1), cut] = block
                    continue
                for q in range(NQ):
                    at = NY * per * q + per * g
                    qr[at : at + per, cut] = block[per * q : per * q + per]
        for j in range(NY):
            lanes = slice(ba * j, ba * j + ba)
            basis = p_ref[j, basis_at:w_at, :]
            for y in range(NY):
                raw = p_ref[y, 2 * seg * j : 2 * seg * (j + 1), :]
                block = jnp.dot(raw, basis, preferred_element_type=F32).astype(BF)
                ta[seg * y : seg * y + seg, lanes] = block[seg:]
                for q in range(NQ):
                    at = NY * per * q + per * y
                    qa[at : at + per, lanes] = block[per * q : per * q + per]
        for q in range(NQ):
            rows = slice(NY * per * q, NY * per * (q + 1))
            moment = lax.dot_general(
                qr[rows, :], qa[rows, :], (((0,), (0,)), ((), ())), preferred_element_type=F32
            )
            for j in range(NY):
                lanes = slice(ba * j, ba * j + ba)
                dm[q % 2, :, lanes] = (moment[:, lanes] * p_ref[j, w_at:, :].astype(F32)).astype(BF)
            proj = jnp.dot(tr[...], dm[q % 2], preferred_element_type=F32)
            total = jnp.zeros((n_tok, ba), F32)
            for j in range(NY):
                lanes = slice(ba * j, ba * j + ba)
                total = total + proj[:, lanes] * ta[:, lanes].astype(F32)
            parts = jnp.sum(total.reshape(half, 2, NZ, seg // NZ, ba), axis=(1, 3))
            for h in range(half):
                ex[q, pl.ds(h, NZ, stride=half), :] = parts[h]
        out_ref[...] = jnp.sum(ex[:, : half * NZ, :], axis=2) * scale

    vmem = pl.BlockSpec(memory_space=pltpu.VMEM)
    return pl.pallas_call(
        body,
        out_shape=pltpu.VMEM((NQ, half * NZ), F32),
        in_specs=[vmem] * 5,
        out_specs=vmem,
        scratch_shapes=[
            pltpu.VMEM((n_tok, fdim), BF),
            pltpu.VMEM((n_tok, fdim), BF),
            pltpu.VMEM((n_tok, ddim), BF),
            pltpu.VMEM((n_tok, ddim), BF),
            pltpu.VMEM((2, fdim, ddim), BF),
            pltpu.VMEM((NQ, half * NZ + 8, ba), F32),
        ],
        name="score",
        compiler_params=pltpu.CompilerParams(vmem_limit_bytes=24 << 20),
        interpret=INTERPRET,
    )(most, rest, b_keep, b_recv, packed)


def local(query_out, query_in, train_out, train_in, basis_out, basis_in, eigvals, owner_map):
    x, y, c = lax.axis_index("x"), lax.axis_index("y"), lax.axis_index("c")
    ba = basis_in.shape[1]
    tok, units = query_out.shape
    width = query_in.shape[1]
    fdim = units // NY
    ddim = NY * ba
    ids = jnp.arange(4, dtype=jnp.int32)
    place = jnp.where(ids == 0, x, jnp.where(ids == 1, y, c)).astype(jnp.int32)

    both_out = jnp.concatenate([query_out, train_out], 0)
    rows = exchange(both_out.reshape(2 * tok, NY, fdim).transpose(1, 0, 2), "y")
    w_keep, w_send, b_keep, b_send = prepare(owner_map, place, eigvals, basis_out)
    q_rows = rows[:, :tok].reshape(NY * tok, fdim)
    t_rows = rows[:, tok:].reshape(NY * tok, fdim)
    n_ag = (NY - 1) * tok

    half_in = jnp.where(c == 0, query_in, train_in)
    cols = half_in.reshape(tok, NZ, ddim).transpose(1, 0, 2)
    last = jnp.broadcast_to(t_rows[None, n_ag:], (NZ, tok, fdim))
    mixed = exchange(jnp.concatenate([cols, last], 1), "z")
    w_own = (w_keep + swap_core(w_send)).reshape(NY, fdim, ba)
    b_recv = swap_core(b_send)
    most = jnp.concatenate([q_rows, t_rows[:n_ag]], 0)
    mixed, most, w_own, b_recv = lax.optimization_barrier((mixed, most, w_own, b_recv))
    rest = mixed[:, tok:].reshape(NZ * tok, fdim)

    in_cols = mixed[:, :tok].reshape(NZ * tok, NY, ba).transpose(1, 0, 2)
    other = swap_core(in_cols)
    pair = jnp.stack([jnp.where(c == 0, in_cols, other), jnp.where(c == 0, other, in_cols)], 1)
    shared = jnp.concatenate([pair.reshape(-1, ba), basis_in[0]], 0)
    shared = jnp.broadcast_to(shared[None], (NY,) + shared.shape)
    packed = exchange(jnp.concatenate([shared, w_own], 1), "y")
    gathered = lax.all_gather(most, "z", axis=0, tiled=True)
    packed, gathered = lax.optimization_barrier((packed, gathered))

    per = NZ * NY * tok // NQ
    hidden = units * NX * NC
    scale = 1.0 / math.sqrt(per * ET * hidden * width)
    scores = score(gathered, rest, b_keep, b_recv, packed, scale)

    flat = scores.reshape(1, -1, 128)
    flat = jnp.sum(exchange(jnp.broadcast_to(flat, (NY * NX * NC,) + flat.shape[1:]), ("y", "x", "c")), axis=0)[None]
    flat = jnp.sum(exchange(jnp.broadcast_to(flat, (NZ,) + flat.shape[1:]), "z"), axis=0)
    return flat.reshape(scores.shape)


def solution(mesh):
    fine = Mesh(mesh.devices.reshape(NZ, NY, NX, NC), ("z", "y", "x", "c"))
    dp, owner = ("z", "y"), ("x", "c")
    in_specs = (
        P(dp, owner),
        P(dp, None),
        P(dp, owner),
        P(dp, None),
        P(owner, None, None),
        P(dp, None, None),
        P(owner, dp),
        P(),
    )
    return jax.shard_map(local, mesh=fine, in_specs=in_specs, out_specs=P(), check_vma=False)
```
